32 devices in a mesh: lat: 8 (over z, y), lon: 4 (over x, core).
Axes of the slice: x: 2, y: 2, z: 4, core: 2. Of those that a mesh axis runs over, the one named last changes fastest.
Arguments:
- grid_fields: bfloat16 [1280, 50, 3, 2560], P('lat', None, None, 'lon'), may hold values from -6 to 6
- legendre: bfloat16 [512, 1280, 640], P(('lat', 'lon')), may hold values from -0.15625 to 0.15625
- wave_of_slot: int32 [512], replicated, may hold values from 0 to 511, as said below
- energy_weight: float32 [3, 640], replicated, may hold values from 0.1 to 10
Outputs:
- spectral: bfloat16 [50, 3, 512, 2, 640], P(None, None, ('lat', 'lon'))
- gram_matrix: float32 [50, 50], replicated
The draws below stay inside these ranges and needn't reach their ends.
Inputs may be any that keep to these rules, and one draw needn't show every extreme that they name: `wave_of_slot`: every wavenumber 0 to 511 stands in exactly one slot; slot d * 16 + r holds a wavenumber of r * 32 to r * 32 + 31.
All inputs are finite; a program needn't handle non-finite values.
Results may differ from the reference program's by a relative error of at most 0.0043.
Values may be sent and summed in bfloat16 or wider, within the bound.
No kernel may reach another device: no remote copies, remote signals or barrier semaphores. Data moves between devices by JAX's collectives and lax.ppermute only.
A program may use at most 256 MiB of HBM per device.

```python
import math
import jax
import jax.numpy as jnp
from jax import lax

NLAT = 1280
NLON = 2560
M = 512
NT = 640
K = 50
LEV = 3
WAVE_ROUND = 32
WAVE_DEV = 16


def draw_wave_of_slot(key, part):

    def draw_round(round_index):
        shuffled = jax.random.permutation(jax.random.fold_in(key, round_index), WAVE_ROUND)
        return shuffled.astype(jnp.int32) + round_index * WAVE_ROUND
    rounds = jax.vmap(draw_round)(jnp.arange(WAVE_DEV, dtype=jnp.int32))
    return rounds.T.reshape(M).astype(jnp.int32)


def shard_levels(stream_key, extent, cuts, least, top_value):
    loudness = 1.0
    for position, parts in cuts:
        heights = jax.random.uniform(jax.random.fold_in(jax.random.fold_in(stream_key, 6), position), (parts,), jnp.float32, least / len(cuts), top_value / len(cuts))
        loudness = loudness * jnp.repeat(jnp.exp(heights), extent[position] // parts).reshape((-1,) + (1,) * (len(extent) - 1 - position))
    return loudness


def scatter_about(own_key, dims, width, most, cuts=(), kind=jnp.bfloat16):
    entries = jax.random.normal(own_key, dims, jnp.float32) * width
    if len(cuts) > 0:
        entries = shard_levels(own_key, dims, cuts, -0.22, 0.18) * entries
    return jnp.clip(entries, min=-most, max=most).astype(kind)


def setup_inputs(seed: int = 0) -> dict:
    keys = jax.random.split(jax.random.key(seed), 5)
    grid_fields = scatter_about(keys[0], (NLAT, K, LEV, NLON), 1.0, 6.0, ((0, 8), (3, 4)))
    legendre = scatter_about(keys[1], (M, NLAT, NT), NLAT ** -0.5, 0.15625, ((0, 32),))
    wave_of_slot = draw_wave_of_slot(jax.random.fold_in(keys[4], 71), 0)
    energy_weight = jnp.clip(jnp.exp(jax.random.uniform(keys[3], (LEV, NT), jnp.float32, math.log(0.1), math.log(10.0))), 0.1, 10.0)
    return dict(grid_fields=grid_fields, legendre=legendre, wave_of_slot=wave_of_slot, energy_weight=energy_weight)


def make_trig(wave_list):
    longitude = jnp.arange(NLON, dtype=jnp.int32)
    phase_index = longitude[:, None] * wave_list.astype(jnp.int32)[None, :] % NLON
    angles = phase_index.astype(jnp.float32) * (2.0 * math.pi / NLON)
    stacked = jnp.stack([jnp.cos(angles), -jnp.sin(angles)], axis=2)
    return stacked.reshape(NLON, 2 * M).astype(jnp.bfloat16)

def reference(grid_fields, legendre, wave_of_slot, energy_weight):
    trig_table = make_trig(wave_of_slot)
    flat_rows = grid_fields.reshape(NLAT * K * LEV, NLON)
    fourier = jnp.dot(flat_rows, trig_table, preferred_element_type=jnp.float32) * (1.0 / math.sqrt(NLON))
    fourier = fourier.reshape(NLAT, K * LEV, M, 2)
    by_slot = jnp.moveaxis(fourier, 2, 0)
    degree_index = jnp.arange(NT, dtype=jnp.int32)
    tri_mask = (degree_index[None, :] >= wave_of_slot[:, None]).astype(jnp.float32)

    def per_slot(items):
        slot_data, slot_table, slot_mask = items
        masked = slot_table.astype(jnp.float32) * slot_mask[None, :]
        return jnp.einsum('afp,an->fpn', slot_data, masked, precision=lax.Precision.HIGHEST)
    full_slots = lax.map(per_slot, (by_slot, legendre, tri_mask))
    full = jnp.moveaxis(full_slots, 0, 1).reshape(K, LEV, M, 2, NT)
    factor = jnp.where(wave_of_slot == 0, 1.0, 2.0).astype(jnp.float32)
    weighted = full * factor[None, None, :, None, None] * energy_weight[None, :, None, None, :]
    gram_matrix = jnp.dot(full.reshape(K, -1), weighted.reshape(K, -1).T, precision=lax.Precision.HIGHEST)
    gram_matrix = gram_matrix / (LEV * M * NT)
    return (full.astype(jnp.bfloat16), gram_matrix)
```

```python
import functools
import math

import jax
import jax.numpy as jnp
from jax import lax
from jax.experimental import pallas as pl
from jax.experimental.pallas import tpu as pltpu
from jax.sharding import Mesh
from jax.sharding import PartitionSpec as P


CORES = 2
LANES = 128
SUB = 8


def make_trig(wave_list, lon_total):
    longitude = jnp.arange(lon_total, dtype=jnp.int32)
    phase_index = longitude[:, None] * wave_list[None, :] % lon_total
    angles = phase_index.astype(jnp.float32) * (2.0 * math.pi / lon_total)
    stacked = jnp.stack([jnp.cos(angles), -jnp.sin(angles)], axis=2)
    return stacked.reshape(lon_total, 2 * wave_list.shape[0]).astype(jnp.bfloat16)


def plain(grid_fields, legendre, wave_of_slot, energy_weight):
    lat_dev, vectors, levels, lon_dev = grid_fields.shape
    bands = lax.axis_size("lat")
    sectors = lax.axis_size("x") * lax.axis_size("core")
    lon_total = lon_dev * sectors
    per_dev = legendre.shape[0]
    degrees = legendre.shape[2]
    fields = vectors * levels
    band_rows = lat_dev // sectors
    norm_scale = 1.0 / math.sqrt(lon_total)
    lon = ("x", "core")
    trig_table = make_trig(wave_of_slot, lon_total)
    moved_rows = lax.all_to_all(grid_fields, lon, split_axis=0, concat_axis=3, tiled=True)
    product = jnp.dot(
        moved_rows.reshape(-1, lon_total), trig_table, preferred_element_type=jnp.float32
    )
    fourier = product.reshape(band_rows, fields, -1) * norm_scale
    gathered = lax.all_to_all(
        lax.all_to_all(fourier, "lat", split_axis=2, concat_axis=0, tiled=True),
        lon,
        split_axis=2,
        concat_axis=0,
        tiled=True,
    )
    cols_here = gathered.shape[2]
    columns = gathered.reshape(sectors, bands, band_rows, fields, cols_here).transpose(
        1, 0, 2, 3, 4
    )
    columns = columns.reshape(bands * lat_dev, fields, per_dev, 2)
    device_slot = lax.axis_index(("lat", "x", "core")) * per_dev
    own_waves = lax.dynamic_slice_in_dim(wave_of_slot, device_slot, per_dev, 0)
    degree_index = jnp.arange(degrees, dtype=jnp.int32)
    tri_mask = (degree_index[None, :] >= own_waves[:, None]).astype(jnp.float32)
    legendre_table = legendre.astype(jnp.float32) * tri_mask[:, None, :]
    spectral = jnp.einsum(
        "aftp,tan->ftpn", columns, legendre_table, precision=lax.Precision.HIGHEST
    )
    spectral = spectral.reshape(vectors, levels, per_dev, 2, degrees)
    factor = jnp.where(own_waves == 0, 1.0, 2.0).astype(jnp.float32)
    weighted = spectral * factor[None, None, :, None, None] * energy_weight[None, :, None, None, :]
    partial_value = jnp.dot(
        spectral.reshape(vectors, -1),
        weighted.reshape(vectors, -1).T,
        precision=lax.Precision.HIGHEST,
    )
    slots = wave_of_slot.shape[0]
    gram_matrix = lax.psum(partial_value, ("lat", "x", "core")) / (levels * slots * degrees)
    return (spectral.astype(jnp.bfloat16), gram_matrix)


class Rows:
    def __init__(self, fields, lat_dev):
        self.fields = fields
        self.rest = lat_dev % LANES
        self.pack = LANES // self.rest
        self.block = self.pack if fields % self.pack == 0 else fields
        self.blocks = fields // self.block
        self.quads_in = -(-self.block // self.pack)
        self.quads = self.blocks * self.quads_in
        self.width = (self.block + self.quads_in) * LANES
        self.total = self.blocks * self.width

    def full(self, f):
        return f // self.block * self.width + f % self.block * LANES

    def tail(self, q):
        return q // self.quads_in * self.width + (self.block + q % self.quads_in) * LANES

    def quad_of(self, f):
        inner = f % self.block
        return f // self.block * self.quads_in + inner // self.pack, inner % self.pack


def fourier_kernel(scale, rows, with_add, *refs):
    if with_add:
        t0, t1, g0, g1, add, out = refs
    else:
        t0, t1, g0, g1, out = refs

    def packed(g):
        parts = [g[f, :LANES, :] for f in range(rows.block)]
        parts += [g[f, LANES:, :] for f in range(rows.block)]
        spare = rows.width - rows.block * g.shape[1]
        if spare:
            parts.append(jnp.zeros((spare, g.shape[2]), g.dtype))
        return jnp.concatenate(parts, axis=0)

    dims = (((1,), (1,)), ((), ()))
    total = lax.dot_general(t0[...], packed(g0), dims, preferred_element_type=jnp.float32)
    total += lax.dot_general(t1[...], packed(g1), dims, preferred_element_type=jnp.float32)
    total *= scale
    if with_add:
        total += add[...].astype(jnp.float32)
    out[...] = total.astype(out.dtype)


def fourier(t0, t1, g0, g1, scale, rows, add=None):
    cols, lon = t0.shape
    lat_dev = g0.shape[1]
    table = pl.BlockSpec((cols, lon), lambda i: (0, 0))
    field = pl.BlockSpec((rows.block, lat_dev, lon), lambda i: (i, 0, 0))
    wide = pl.BlockSpec((cols, rows.width), lambda i: (0, i))
    args = [t0, t1, g0, g1] + ([] if add is None else [add])
    return pl.pallas_call(
        functools.partial(fourier_kernel, scale, rows, add is not None),
        grid=(rows.blocks,),
        in_specs=[table, table, field, field] + ([] if add is None else [wide]),
        out_specs=wide,
        out_shape=jax.ShapeDtypeStruct((cols, rows.total), jnp.bfloat16),
        compiler_params=pltpu.CompilerParams(vmem_limit_bytes=48 * 2**20),
        cost_estimate=pl.CostEstimate(
            flops=4 * cols * rows.total * lon,
            bytes_accessed=4 * rows.total * lon + 4 * cols * rows.total + 4 * cols * lon,
            transcendentals=0,
        ),
        name="fourier",
    )(*args)


def legendre_kernel(bands, rows, lat_dev, degrees, cof, leg, wave, out):
    fields, pack, rest = rows.fields, rows.pack, rows.rest
    lane = lax.broadcasted_iota(jnp.int32, (CORES * rows.quads * SUB, LANES), 1) // rest

    def stacked(z, starts):
        parts = [
            cof[z * CORES + c, :, at : at + LANES].astype(jnp.float32)
            for c in range(CORES)
            for at in starts
        ]
        return jnp.concatenate(parts, axis=0)

    left = [stacked(z, [rows.full(f) for f in range(fields)]) for z in range(bands)]
    for g in range(bands // pack):
        shards = [None] * pack
        for slot in range(pack):
            tail = stacked(g * pack + slot, [rows.tail(q) for q in range(rows.quads)])
            for j in range(pack):
                shift = (slot - j) % pack * rest
                moved = tail if shift == 0 else pltpu.roll(tail, shift, 1)
                shards[j] = moved if slot == 0 else jnp.where(lane == slot, moved, shards[j])
        pieces = []
        for c in range(CORES):
            for f in range(fields):
                quad, j = rows.quad_of(f)
                at = (c * rows.quads + quad) * SUB
                pieces.append(shards[j][at : at + SUB])
        left.append(jnp.concatenate(pieces, axis=0))
    count = CORES * fields * SUB
    left = jnp.concatenate(left, axis=1)
    slot_of_row = lax.broadcasted_iota(jnp.int32, (count, 1), 0) % SUB // 2
    total = jnp.zeros((count, degrees), jnp.float32)
    for s in range(SUB // 2):
        here = jnp.where(slot_of_row == s, left, 0.0).astype(jnp.bfloat16)
        table = jnp.concatenate(
            [leg[s, z * lat_dev : z * lat_dev + LANES, :] for z in range(bands)]
            + [leg[s, z * lat_dev + LANES : (z + 1) * lat_dev, :] for z in range(bands)],
            axis=0,
        )
        total += jnp.dot(here, table, preferred_element_type=jnp.float32)
    total = total.reshape(CORES * fields, SUB, degrees)
    degree = lax.broadcasted_iota(jnp.int32, (SUB, degrees), 1)
    keep = degree >= wave[:, :1]
    total = jnp.where(keep[None], total, 0.0)
    out[...] = total.astype(out.dtype)


def legendre_sums(cof, leg, waves, rows):
    sources, slot_rows, _ = cof.shape
    fields = rows.fields
    slots, lats, degrees = leg.shape
    bands = sources // CORES
    lat_dev = lats // bands
    return pl.pallas_call(
        functools.partial(legendre_kernel, bands, rows, lat_dev, degrees),
        grid=(slot_rows // SUB,),
        in_specs=[
            pl.BlockSpec((sources, SUB, rows.total), lambda i: (0, i, 0)),
            pl.BlockSpec((SUB // 2, lats, degrees), lambda i: (i, 0, 0)),
            pl.BlockSpec((SUB, LANES), lambda i: (i, 0)),
        ],
        out_specs=pl.BlockSpec((CORES * fields, SUB, degrees), lambda i: (0, i, 0)),
        out_shape=jax.ShapeDtypeStruct((CORES * fields, slot_rows, degrees), jnp.bfloat16),
        compiler_params=pltpu.CompilerParams(vmem_limit_bytes=56 * 2**20),
        cost_estimate=pl.CostEstimate(
            flops=4 * CORES * fields * slot_rows * lats * degrees,
            bytes_accessed=2 * sources * slot_rows * rows.total + 2 * slots * lats * degrees,
            transcendentals=0,
        ),
        name="legendre",
    )(cof, leg, waves)


def gram_kernel(groups, *refs):
    specs = refs[:groups]
    weight, wave, place, out, total = refs[groups:]
    step = pl.program_id(0) * pl.num_programs(1) + pl.program_id(1)
    values = jnp.concatenate([r[...].reshape(-1, r.shape[-1]) for r in specs], axis=0)
    rows, degrees = values.shape
    vectors = rows // SUB
    factor = jnp.where(wave[:, :1] == 0, 1.0, 2.0).astype(jnp.float32)
    scaled = values.astype(jnp.float32).reshape(vectors, SUB, degrees) * (factor * weight[0])[None]
    scaled = scaled.reshape(rows, degrees).astype(jnp.bfloat16)
    part = lax.dot_general(
        scaled, values, (((1,), (1,)), ((), ())), preferred_element_type=jnp.float32
    )

    @pl.when(step == 0)
    def _():
        total[...] = part

    @pl.when(step > 0)
    def _():
        total[...] += part

    @pl.when(step == pl.num_programs(0) * pl.num_programs(1) - 1)
    def _():
        row = lax.broadcasted_iota(jnp.int32, (rows, rows), 0)
        col = lax.broadcasted_iota(jnp.int32, (rows, rows), 1)
        kept = jnp.where(row % SUB == col % SUB, total[...], 0.0)
        slot = lax.broadcasted_iota(jnp.int32, (vectors, rows), 0)
        pick = (place[:1, :] == slot).astype(jnp.float32)
        half = jnp.dot(
            pick, kept, preferred_element_type=jnp.float32, precision=lax.Precision.HIGHEST
        )
        out[...] = lax.dot_general(
            half,
            pick,
            (((1,), (1,)), ((), ())),
            preferred_element_type=jnp.float32,
            precision=lax.Precision.HIGHEST,
        )


def gram_sums(specs, order, weight, waves):
    _, levels, slot_rows, degrees = specs[0].shape
    vectors = len(order)
    place = jnp.repeat(jnp.asarray(order, jnp.int32), SUB)
    place = jnp.broadcast_to(place[None], (SUB, vectors * SUB))
    return pl.pallas_call(
        functools.partial(gram_kernel, len(specs)),
        grid=(levels, slot_rows // SUB),
        in_specs=[
            pl.BlockSpec((s.shape[0], 1, SUB, degrees), lambda l, i: (0, l, i, 0)) for s in specs
        ]
        + [
            pl.BlockSpec((1, 1, degrees), lambda l, i: (l, 0, 0)),
            pl.BlockSpec((SUB, LANES), lambda l, i: (i, 0)),
            pl.BlockSpec((SUB, vectors * SUB), lambda l, i: (0, 0)),
        ],
        out_specs=pl.BlockSpec((vectors, vectors), lambda l, i: (0, 0)),
        out_shape=jax.ShapeDtypeStruct((vectors, vectors), jnp.float32),
        scratch_shapes=[pltpu.VMEM((vectors * SUB, vectors * SUB), jnp.float32)],
        compiler_params=pltpu.CompilerParams(vmem_limit_bytes=48 * 2**20),
        name="gram",
    )(*specs, weight.reshape(levels, 1, degrees), waves, place)


def chunk_sizes(half):
    ends = [2] if half > 12 else []
    tail = [2, 1] if half > 12 else []
    left = half - sum(ends) - sum(tail)
    middle = [4] * (left // 4) + ([left % 4] if left % 4 else [])
    return ends + middle + tail


def cosine(turn, total):
    turn = turn.astype(jnp.float32)
    quadrant = jnp.floor(turn * (4.0 / total) + 0.5)
    angle = (turn - quadrant * (total / 4.0)) * (2.0 * math.pi / total)
    square = angle * angle
    even = 1.0 + square * (-1 / 2 + square * (1 / 24 + square * (-1 / 720 + square / 40320)))
    odd = 1.0 + square * (-1 / 6 + square * (1 / 120 + square * (-1 / 5040 + square / 362880)))
    quadrant = quadrant.astype(jnp.int32)
    value = jnp.where(quadrant % 2 == 0, even, angle * odd)
    return jnp.where((quadrant + 1) % 4 < 2, value, -value)


def make_tables(wave_of_slot, bands, per_dev, lon_dev, lon_total):
    xs = lax.axis_size("x")
    my_x = lax.axis_index("x")
    my_core = lax.axis_index("core")
    waves = wave_of_slot.reshape(bands, xs, CORES * per_dev).transpose(1, 0, 2).reshape(xs, -1)
    waves = jnp.roll(waves, -my_x, axis=0)
    quarter = jnp.arange(waves.shape[1] * 2, dtype=jnp.int32) % 2 * (lon_total // 4)
    longitude = jnp.arange(lon_dev, dtype=jnp.int32)
    tables = []
    for core in (my_core, 1 - my_core):
        here = (my_x * CORES + core) * lon_dev + longitude
        tables.append(
            [
                cosine(
                    jnp.repeat(waves[step], 2)[:, None] * here[None, :] + quarter[:, None],
                    lon_total,
                ).astype(jnp.bfloat16)
                for step in range(xs)
            ]
        )
    return tables


def fast(grid_fields, legendre, wave_of_slot, energy_weight):
    lat_dev, vectors, levels, lon_dev = grid_fields.shape
    bands = lax.axis_size("lat")
    xs = lax.axis_size("x")
    lon_total = lon_dev * xs * CORES
    per_dev, _, degrees = legendre.shape
    slots = wave_of_slot.shape[0]
    scale = 1.0 / math.sqrt(lon_total)
    half = vectors // CORES
    my_core = lax.axis_index("core")
    by_field = grid_fields.transpose(1, 2, 0, 3).reshape(vectors * levels, lat_dev, lon_dev)
    swap = [(0, 1), (1, 0)]
    sizes = chunk_sizes(half)
    starts = [sum(sizes[:i]) for i in range(len(sizes))]

    tables = make_tables(wave_of_slot, bands, per_dev, lon_dev, lon_total)
    device_slot = lax.axis_index(("lat", "x", "core")) * per_dev
    own_waves = lax.dynamic_slice_in_dim(wave_of_slot, device_slot, per_dev, 0)
    wave_rows = jnp.broadcast_to(jnp.repeat(own_waves, 2)[:, None], (2 * per_dev, LANES))

    done = []
    order = []
    for count, offset in zip(sizes, starts, strict=True):
        rows = Rows(count * levels, lat_dev)

        def fields_of(core, offset=offset, rows=rows):
            first = (core * half + offset) * levels
            return lax.dynamic_slice_in_dim(by_field, first, rows.fields, 0)

        own = fields_of(my_core)
        came = lax.ppermute(fields_of(1 - my_core), "core", swap)
        add = None
        for step in range(1, xs):
            there = fourier(tables[0][step], tables[1][step], own, came, scale, rows)
            part = lax.ppermute(there, "x", [(j, (j + step) % xs) for j in range(xs)])
            add = part if xs == 2 else part.astype(jnp.float32) + (0.0 if add is None else add)
        mine = fourier(tables[0][0], tables[1][0], own, came, scale, rows, add)
        mine = mine.reshape(bands * CORES, 2 * per_dev, -1)
        cof = lax.all_to_all(mine, ("lat", "core"), 0, 0, tiled=True)
        sums = legendre_sums(cof, legendre, wave_rows, rows)
        done.append(sums.reshape(CORES * count, levels, 2 * per_dev, degrees))
        order += [c * half + offset + k for c in range(CORES) for k in range(count)]
    shape = (CORES, -1, levels, per_dev, 2, degrees)
    spectral = jnp.concatenate([d.reshape(shape) for d in done], axis=1)
    partial_value = gram_sums(done, order, energy_weight, wave_rows)
    parts = lax.all_gather(partial_value, ("lat", "x", "core"))
    gram_matrix = jnp.sum(parts, axis=0) / (levels * slots * degrees)
    return (spectral.reshape(vectors, levels, per_dev, 2, degrees), gram_matrix)


def on_device(grid_fields, legendre, wave_of_slot, energy_weight):
    lat_dev, vectors, _, lon_dev = grid_fields.shape
    bands = lax.axis_size("lat")
    rest = lat_dev % LANES
    fits = (
        lat_dev // LANES == 1
        and rest >= 16
        and LANES % rest == 0
        and bands % (LANES // rest) == 0
        and legendre.shape[0] * 2 % SUB == 0
        and vectors % CORES == 0
        and lon_dev % LANES == 0
    )
    body = fast if fits else plain
    return body(grid_fields, legendre, wave_of_slot, energy_weight)


def solution(mesh):
    lat, lon = mesh.devices.shape
    wide = Mesh(mesh.devices.reshape(lat, lon // CORES, CORES), ("lat", "x", "core"))
    lons = ("x", "core")
    placed = (P("lat", None, None, lons), P(("lat", "x", "core"), None, None), P(), P())
    return jax.shard_map(
        on_device,
        mesh=wide,
        in_specs=placed,
        out_specs=(P(None, None, ("lat", "x", "core"), None, None), P()),
        check_vma=False,
    )
```

```python
import functools
import math

import jax
import jax.numpy as jnp
from jax import lax
from jax.experimental import pallas as pl
from jax.experimental.pallas import tpu as pltpu
from jax.sharding import Mesh
from jax.sharding import PartitionSpec as P


CORES = 2
LANES = 128
SUB = 8
VMEM = 58 * 2**20


def make_trig(wave_list, lon_total):
    longitude = jnp.arange(lon_total, dtype=jnp.int32)
    phase_index = longitude[:, None] * wave_list[None, :] % lon_total
    angles = phase_index.astype(jnp.float32) * (2.0 * math.pi / lon_total)
    stacked = jnp.stack([jnp.cos(angles), -jnp.sin(angles)], axis=2)
    return stacked.reshape(lon_total, 2 * wave_list.shape[0]).astype(jnp.bfloat16)


def plain(grid_fields, legendre, wave_of_slot, energy_weight):
    lat_dev, vectors, levels, lon_dev = grid_fields.shape
    bands = lax.axis_size("lat")
    sectors = lax.axis_size("x") * lax.axis_size("core")
    lon_total = lon_dev * sectors
    per_dev = legendre.shape[0]
    degrees = legendre.shape[2]
    fields = vectors * levels
    band_rows = lat_dev // sectors
    norm_scale = 1.0 / math.sqrt(lon_total)
    lon = ("x", "core")
    trig_table = make_trig(wave_of_slot, lon_total)
    moved_rows = lax.all_to_all(grid_fields, lon, split_axis=0, concat_axis=3, tiled=True)
    product = jnp.dot(
        moved_rows.reshape(-1, lon_total), trig_table, preferred_element_type=jnp.float32
    )
    fourier = product.reshape(band_rows, fields, -1) * norm_scale
    gathered = lax.all_to_all(
        lax.all_to_all(fourier, "lat", split_axis=2, concat_axis=0, tiled=True),
        lon,
        split_axis=2,
        concat_axis=0,
        tiled=True,
    )
    cols_here = gathered.shape[2]
    columns = gathered.reshape(sectors, bands, band_rows, fields, cols_here).transpose(
        1, 0, 2, 3, 4
    )
    columns = columns.reshape(bands * lat_dev, fields, per_dev, 2)
    device_slot = lax.axis_index(("lat", "x", "core")) * per_dev
    own_waves = lax.dynamic_slice_in_dim(wave_of_slot, device_slot, per_dev, 0)
    degree_index = jnp.arange(degrees, dtype=jnp.int32)
    tri_mask = (degree_index[None, :] >= own_waves[:, None]).astype(jnp.float32)
    legendre_table = legendre.astype(jnp.float32) * tri_mask[:, None, :]
    spectral = jnp.einsum(
        "aftp,tan->ftpn", columns, legendre_table, precision=lax.Precision.HIGHEST
    )
    spectral = spectral.reshape(vectors, levels, per_dev, 2, degrees)
    factor = jnp.where(own_waves == 0, 1.0, 2.0).astype(jnp.float32)
    weighted = spectral * factor[None, None, :, None, None] * energy_weight[None, :, None, None, :]
    partial_value = jnp.dot(
        spectral.reshape(vectors, -1),
        weighted.reshape(vectors, -1).T,
        precision=lax.Precision.HIGHEST,
    )
    slots = wave_of_slot.shape[0]
    gram_matrix = lax.psum(partial_value, ("lat", "x", "core")) / (levels * slots * degrees)
    return (spectral.astype(jnp.bfloat16), gram_matrix)


class Rows:
    def __init__(self, fields, lat_dev):
        self.fields = fields
        self.rest = lat_dev % LANES
        self.pack = LANES // self.rest
        self.block = self.pack if fields % self.pack == 0 else fields
        self.blocks = fields // self.block
        self.quads_in = -(-self.block // self.pack)
        self.quads = self.blocks * self.quads_in
        self.width = (self.block + self.quads_in) * LANES
        self.total = self.blocks * self.width

    def full(self, f):
        return f // self.block * self.width + f % self.block * LANES

    def tail(self, q):
        return q // self.quads_in * self.width + (self.block + q % self.quads_in) * LANES

    def quad_of(self, f):
        inner = f % self.block
        return f // self.block * self.quads_in + inner // self.pack, inner % self.pack


def fourier_kernel(scale, rows, with_add, first, *refs):
    own = refs[: rows.block]
    if with_add:
        t0, t1, other, add, out = refs[rows.block :]
    else:
        t0, t1, other, out = refs[rows.block :]
    spare = rows.width - rows.block * other.shape[1]
    zero = [jnp.zeros((spare, other.shape[2]), other.dtype)] if spare else []
    whole = range(rows.block)
    g0 = [own[f][0, :LANES, :] for f in whole] + [own[f][0, LANES:, :] for f in whole]
    g1 = [other[f, :LANES, :] for f in whole] + [other[f, LANES:, :] for f in whole]
    dims = (((1,), (1,)), ((), ()))
    g0 = jnp.concatenate(g0 + zero, axis=0)
    g1 = jnp.concatenate(g1 + zero, axis=0)
    total = lax.dot_general(t0[...], g0, dims, preferred_element_type=jnp.float32)
    total += lax.dot_general(t1[...], g1, dims, preferred_element_type=jnp.float32)
    total *= scale
    if with_add:
        total += add[...].astype(jnp.float32)
    out[...] = total.astype(out.dtype)


def fourier(t0, t1, by_field, first, other, scale, rows, add=None):
    cols, lon = t0.shape
    lat_dev = other.shape[1]
    table = pl.BlockSpec((cols, lon), lambda i, at: (0, 0))
    own = [
        pl.BlockSpec((1, lat_dev, lon), lambda i, at, f=f: (at[0] + i * rows.block + f, 0, 0))
        for f in range(rows.block)
    ]
    field = pl.BlockSpec((rows.block, lat_dev, lon), lambda i, at: (i, 0, 0))
    wide = pl.BlockSpec((cols, rows.width), lambda i, at: (0, i))
    adds = [] if add is None else [add]
    return pl.pallas_call(
        functools.partial(fourier_kernel, scale, rows, add is not None),
        grid_spec=pltpu.PrefetchScalarGridSpec(
            num_scalar_prefetch=1,
            grid=(rows.blocks,),
            in_specs=own + [table, table, field] + [wide for _ in adds],
            out_specs=wide,
        ),
        out_shape=jax.ShapeDtypeStruct((cols, rows.total), jnp.bfloat16),
        compiler_params=pltpu.CompilerParams(vmem_limit_bytes=VMEM),
        cost_estimate=pl.CostEstimate(
            flops=4 * cols * rows.total * lon,
            bytes_accessed=4 * rows.total * lon + 4 * cols * rows.total + 4 * cols * lon,
            transcendentals=0,
        ),
        name="fourier",
    )(first.reshape(1), *[by_field] * rows.block, t0, t1, other, *adds)


def left_rows(bands, rows, cof):
    fields, pack, rest = rows.fields, rows.pack, rows.rest
    lane = lax.broadcasted_iota(jnp.int32, (CORES * rows.quads * SUB, LANES), 1) // rest

    def stacked(z, starts):
        parts = [
            cof[z * CORES + c, :, at : at + LANES].astype(jnp.float32)
            for c in range(CORES)
            for at in starts
        ]
        return jnp.concatenate(parts, axis=0)

    left = [stacked(z, [rows.full(f) for f in range(fields)]) for z in range(bands)]
    for g in range(bands // pack):
        shards = [None] * pack
        for slot in range(pack):
            tail = stacked(g * pack + slot, [rows.tail(q) for q in range(rows.quads)])
            for j in range(pack):
                shift = (slot - j) % pack * rest
                moved = tail if shift == 0 else pltpu.roll(tail, shift, 1)
                shards[j] = moved if slot == 0 else jnp.where(lane == slot, moved, shards[j])
        pieces = []
        for c in range(CORES):
            for f in range(fields):
                quad, j = rows.quad_of(f)
                at = (c * rows.quads + quad) * SUB
                pieces.append(shards[j][at : at + SUB])
        left.append(jnp.concatenate(pieces, axis=0))
    return jnp.concatenate(left, axis=1)


def legendre_kernel(bands, chunks, lat_dev, degrees, *refs):
    cofs = refs[: len(chunks)]
    leg, wave = refs[len(chunks) : len(chunks) + 2]
    outs = refs[len(chunks) + 2 :]
    left = [left_rows(bands, rows, cof) for rows, cof in zip(chunks, cofs, strict=True)]
    left = jnp.concatenate(left, axis=0)
    count = left.shape[0]
    slot_of_row = lax.broadcasted_iota(jnp.int32, (count, 1), 0) % SUB // 2
    total = jnp.zeros((count, degrees), jnp.float32)
    for s in range(SUB // 2):
        here = jnp.where(slot_of_row == s, left, 0.0).astype(jnp.bfloat16)
        table = jnp.concatenate(
            [leg[s, z * lat_dev : z * lat_dev + LANES, :] for z in range(bands)]
            + [leg[s, z * lat_dev + LANES : (z + 1) * lat_dev, :] for z in range(bands)],
            axis=0,
        )
        total += jnp.dot(here, table, preferred_element_type=jnp.float32)
    total = total.reshape(count // SUB, SUB, degrees)
    degree = lax.broadcasted_iota(jnp.int32, (SUB, degrees), 1)
    keep = degree >= wave[:, :1]
    total = jnp.where(keep[None], total, 0.0)
    at = 0
    for out in outs:
        out[...] = total[at : at + out.shape[0]].astype(out.dtype)
        at += out.shape[0]


def legendre_sums(cofs, chunks, leg, waves):
    sources, slot_rows, _ = cofs[0].shape
    slots, lats, degrees = leg.shape
    bands = sources // CORES
    lat_dev = lats // bands
    counts = [CORES * rows.fields for rows in chunks]
    total = sum(rows.total for rows in chunks)
    return pl.pallas_call(
        functools.partial(legendre_kernel, bands, chunks, lat_dev, degrees),
        grid=(slot_rows // SUB,),
        in_specs=[pl.BlockSpec((sources, SUB, rows.total), lambda i: (0, i, 0)) for rows in chunks]
        + [
            pl.BlockSpec((SUB // 2, lats, degrees), lambda i: (i, 0, 0)),
            pl.BlockSpec((SUB, LANES), lambda i: (i, 0)),
        ],
        out_specs=[pl.BlockSpec((n, SUB, degrees), lambda i: (0, i, 0)) for n in counts],
        out_shape=[jax.ShapeDtypeStruct((n, slot_rows, degrees), jnp.bfloat16) for n in counts],
        compiler_params=pltpu.CompilerParams(vmem_limit_bytes=VMEM),
        cost_estimate=pl.CostEstimate(
            flops=4 * sum(counts) * slot_rows * lats * degrees,
            bytes_accessed=2 * sources * slot_rows * total + 2 * slots * lats * degrees,
            transcendentals=0,
        ),
        name="legendre",
    )(*cofs, leg, waves)


def gram_kernel(groups, *refs):
    specs = refs[:groups]
    weight, wave, place, out, total = refs[groups:]
    step = pl.program_id(0) * pl.num_programs(1) + pl.program_id(1)
    values = jnp.concatenate([r[...].reshape(-1, r.shape[-1]) for r in specs], axis=0)
    rows, degrees = values.shape
    vectors = rows // SUB
    factor = jnp.where(wave[:, :1] == 0, 1.0, 2.0).astype(jnp.float32)
    scaled = values.astype(jnp.float32).reshape(vectors, SUB, degrees) * (factor * weight[0])[None]
    scaled = scaled.reshape(rows, degrees).astype(jnp.bfloat16)
    part = lax.dot_general(
        scaled, values, (((1,), (1,)), ((), ())), preferred_element_type=jnp.float32
    )

    @pl.when(step == 0)
    def _():
        total[...] = part

    @pl.when(step > 0)
    def _():
        total[...] += part

    @pl.when(step == pl.num_programs(0) * pl.num_programs(1) - 1)
    def _():
        row = lax.broadcasted_iota(jnp.int32, (rows, rows), 0)
        col = lax.broadcasted_iota(jnp.int32, (rows, rows), 1)
        kept = jnp.where(row % SUB == col % SUB, total[...], 0.0)
        slot = lax.broadcasted_iota(jnp.int32, (vectors, rows), 0)
        pick = (place[:1, :] == slot).astype(jnp.float32)
        half = jnp.dot(
            pick, kept, preferred_element_type=jnp.float32, precision=lax.Precision.HIGHEST
        )
        out[...] = lax.dot_general(
            half,
            pick,
            (((1,), (1,)), ((), ())),
            preferred_element_type=jnp.float32,
            precision=lax.Precision.HIGHEST,
        )


def gram_sums(specs, order, weight, waves):
    _, levels, slot_rows, degrees = specs[0].shape
    vectors = len(order)
    place = jnp.repeat(jnp.asarray(order, jnp.int32), SUB)
    place = jnp.broadcast_to(place[None], (SUB, vectors * SUB))
    return pl.pallas_call(
        functools.partial(gram_kernel, len(specs)),
        grid=(levels, slot_rows // SUB),
        in_specs=[
            pl.BlockSpec((s.shape[0], 1, SUB, degrees), lambda l, i: (0, l, i, 0)) for s in specs
        ]
        + [
            pl.BlockSpec((1, 1, degrees), lambda l, i: (l, 0, 0)),
            pl.BlockSpec((SUB, LANES), lambda l, i: (i, 0)),
            pl.BlockSpec((SUB, vectors * SUB), lambda l, i: (0, 0)),
        ],
        out_specs=pl.BlockSpec((vectors, vectors), lambda l, i: (0, 0)),
        out_shape=jax.ShapeDtypeStruct((vectors, vectors), jnp.float32),
        scratch_shapes=[pltpu.VMEM((vectors * SUB, vectors * SUB), jnp.float32)],
        compiler_params=pltpu.CompilerParams(vmem_limit_bytes=VMEM),
        name="gram",
    )(*specs, weight.reshape(levels, 1, degrees), waves, place)


def chunk_sizes(half, quad):
    first = half % quad
    return ([first] if first else []) + [quad] * (half // quad)


def groups_of(count):
    pairs = [list(range(i, min(i + 2, count - 1))) for i in range(0, count - 1, 2)]
    return pairs + [[count - 1]]


def cosine(turn, total):
    inside = turn - jnp.floor(turn * (1.0 / total) + 0.5) * total
    angle = inside * (2.0 * math.pi / total)
    square = angle * angle
    value = 1.0 / math.factorial(18)
    for k in range(8, -1, -1):
        value = 1.0 / math.factorial(2 * k) - square * value
    return value


def make_tables(waves, here, lon_total):
    part = jnp.arange(waves.shape[0] * 2, dtype=jnp.int32) % 2
    quarter = part.astype(jnp.float32) * (lon_total / 4.0)
    turn = jnp.repeat(waves, 2).astype(jnp.float32)[:, None] * here[None, :] + quarter[:, None]
    return cosine(turn, float(lon_total)).astype(jnp.bfloat16)


def all_sum(value):
    for axis in ("core", "x", "lat"):
        size = lax.axis_size(axis)
        step = 1
        while step < size:
            value = value + lax.ppermute(value, axis, [(i, i ^ step) for i in range(size)])
            step *= 2
    return value


def after(value, other):
    return lax.optimization_barrier((value, other))[0]


def fast(grid_fields, legendre, wave_of_slot, energy_weight):
    lat_dev, vectors, levels, lon_dev = grid_fields.shape
    bands = lax.axis_size("lat")
    xs = lax.axis_size("x")
    lon_total = lon_dev * xs * CORES
    per_dev, _, degrees = legendre.shape
    slots = wave_of_slot.shape[0]
    scale = 1.0 / math.sqrt(lon_total)
    half = vectors // CORES
    my_core = lax.axis_index("core")
    my_x = lax.axis_index("x")
    by_field = grid_fields.transpose(1, 2, 0, 3).reshape(vectors * levels, lat_dev, lon_dev)
    swap = [(0, 1), (1, 0)]
    pack = LANES // (lat_dev % LANES)
    sizes = chunk_sizes(half, pack // math.gcd(pack, levels))
    starts = [sum(sizes[:i]) for i in range(len(sizes))]
    chunks = [Rows(size * levels, lat_dev) for size in sizes]
    groups = groups_of(len(sizes))

    waves = wave_of_slot.reshape(bands, xs, CORES * per_dev).transpose(1, 0, 2).reshape(xs, -1)
    waves = jnp.roll(waves, -my_x, axis=0)
    longitude = jnp.arange(lon_dev, dtype=jnp.int32)
    sectors = [
        ((my_x * CORES + core) * lon_dev + longitude).astype(jnp.float32)
        for core in (my_core, 1 - my_core)
    ]
    tables = {s: [make_tables(waves[s], here, lon_total) for here in sectors] for s in range(1, xs)}
    device_slot = lax.axis_index(("lat", "x", "core")) * per_dev
    own_waves = lax.dynamic_slice_in_dim(wave_of_slot, device_slot, per_dev, 0)
    wave_rows = jnp.broadcast_to(jnp.repeat(own_waves, 2)[:, None], (2 * per_dev, LANES))

    sent = []
    cofs = []
    done = {}
    for i, rows in enumerate(chunks):
        first = (my_core * half + starts[i]) * levels
        away = ((1 - my_core) * half + starts[i]) * levels
        if sent:
            away = after(away, sent[max(i - 2, 0)])
        away = lax.dynamic_slice_in_dim(by_field, away, rows.fields, 0)
        came = lax.ppermute(away, "core", swap)
        add = None
        for step in range(1, xs):
            there = fourier(*tables[step], by_field, first, came, scale, rows)
            part = lax.ppermute(there, "x", [(j, (j + step) % xs) for j in range(xs)])
            add = part if xs == 2 else part.astype(jnp.float32) + (0.0 if add is None else add)
        if not sent:
            own_set = after(waves[0], there)
            tables[0] = [make_tables(own_set, here, lon_total) for here in sectors]
        sent.append(there)
        mine = fourier(*tables[0], by_field, first, came, scale, rows, add)
        mine = mine.reshape(bands * CORES, 2 * per_dev, -1)
        if cofs:
            mine = after(mine, cofs[-1])
        cofs.append(lax.all_to_all(mine, ("lat", "core"), 0, 0, tiled=True))
        for group in groups:
            if group[-1] == i:
                sums = legendre_sums(
                    [cofs[j] for j in group], [chunks[j] for j in group], legendre, wave_rows
                )
                for j, value in zip(group, sums, strict=True):
                    done[j] = value.reshape(-1, levels, 2 * per_dev, degrees)
    done = [done[i] for i in range(len(chunks))]
    order = [
        c * half + start + k
        for size, start in zip(sizes, starts, strict=True)
        for c in range(CORES)
        for k in range(size)
    ]
    shape = (CORES, -1, levels, per_dev, 2, degrees)
    spectral = jnp.concatenate([d.reshape(shape) for d in done], axis=1)
    partial_value = gram_sums(done, order, energy_weight, wave_rows)
    gram_matrix = all_sum(partial_value) / (levels * slots * degrees)
    return (spectral.reshape(vectors, levels, per_dev, 2, degrees), gram_matrix)


def on_device(grid_fields, legendre, wave_of_slot, energy_weight):
    lat_dev, vectors, _, lon_dev = grid_fields.shape
    bands = lax.axis_size("lat")
    rest = lat_dev % LANES
    fits = (
        lat_dev // LANES == 1
        and rest >= 16
        and LANES % rest == 0
        and bands % (LANES // rest) == 0
        and legendre.shape[0] * 2 % SUB == 0
        and vectors % CORES == 0
        and lon_dev % LANES == 0
        and wave_of_slot.shape[0] * lon_dev * lax.axis_size("x") * CORES < 2**23
        and lax.axis_size("x") > 1
        and all(lax.axis_size(a) & (lax.axis_size(a) - 1) == 0 for a in ("lat", "x", "core"))
    )
    body = fast if fits else plain
    return body(grid_fields, legendre, wave_of_slot, energy_weight)


def solution(mesh):
    lat, lon = mesh.devices.shape
    wide = Mesh(mesh.devices.reshape(lat, lon // CORES, CORES), ("lat", "x", "core"))
    lons = ("x", "core")
    placed = (P("lat", None, None, lons), P(("lat", "x", "core"), None, None), P(), P())
    return jax.shard_map(
        on_device,
        mesh=wide,
        in_specs=placed,
        out_specs=(P(None, None, ("lat", "x", "core"), None, None), P()),
        check_vma=False,
    )
```

```python
import functools
import math

import jax
import jax.numpy as jnp
from jax import lax
from jax.experimental import pallas as pl
from jax.experimental.pallas import tpu as pltpu
from jax.sharding import Mesh
from jax.sharding import PartitionSpec as P


CORES = 2
LANES = 128
SUB = 8
VMEM = 58 * 2**20


def make_trig(wave_list, lon_total):
    longitude = jnp.arange(lon_total, dtype=jnp.int32)
    phase_index = longitude[:, None] * wave_list[None, :] % lon_total
    angles = phase_index.astype(jnp.float32) * (2.0 * math.pi / lon_total)
    stacked = jnp.stack([jnp.cos(angles), -jnp.sin(angles)], axis=2)
    return stacked.reshape(lon_total, 2 * wave_list.shape[0]).astype(jnp.bfloat16)


def plain(grid_fields, legendre, wave_of_slot, energy_weight):
    lat_dev, vectors, levels, lon_dev = grid_fields.shape
    bands = lax.axis_size("lat")
    sectors = lax.axis_size("x") * lax.axis_size("core")
    lon_total = lon_dev * sectors
    per_dev = legendre.shape[0]
    degrees = legendre.shape[2]
    fields = vectors * levels
    band_rows = lat_dev // sectors
    norm_scale = 1.0 / math.sqrt(lon_total)
    lon = ("x", "core")
    trig_table = make_trig(wave_of_slot, lon_total)
    moved_rows = lax.all_to_all(grid_fields, lon, split_axis=0, concat_axis=3, tiled=True)
    product = jnp.dot(
        moved_rows.reshape(-1, lon_total), trig_table, preferred_element_type=jnp.float32
    )
    fourier = product.reshape(band_rows, fields, -1) * norm_scale
    gathered = lax.all_to_all(
        lax.all_to_all(fourier, "lat", split_axis=2, concat_axis=0, tiled=True),
        lon,
        split_axis=2,
        concat_axis=0,
        tiled=True,
    )
    cols_here = gathered.shape[2]
    columns = gathered.reshape(sectors, bands, band_rows, fields, cols_here).transpose(
        1, 0, 2, 3, 4
    )
    columns = columns.reshape(bands * lat_dev, fields, per_dev, 2)
    device_slot = lax.axis_index(("lat", "x", "core")) * per_dev
    own_waves = lax.dynamic_slice_in_dim(wave_of_slot, device_slot, per_dev, 0)
    degree_index = jnp.arange(degrees, dtype=jnp.int32)
    tri_mask = (degree_index[None, :] >= own_waves[:, None]).astype(jnp.float32)
    legendre_table = legendre.astype(jnp.float32) * tri_mask[:, None, :]
    spectral = jnp.einsum(
        "aftp,tan->ftpn", columns, legendre_table, precision=lax.Precision.HIGHEST
    )
    spectral = spectral.reshape(vectors, levels, per_dev, 2, degrees)
    factor = jnp.where(own_waves == 0, 1.0, 2.0).astype(jnp.float32)
    weighted = spectral * factor[None, None, :, None, None] * energy_weight[None, :, None, None, :]
    partial_value = jnp.dot(
        spectral.reshape(vectors, -1),
        weighted.reshape(vectors, -1).T,
        precision=lax.Precision.HIGHEST,
    )
    slots = wave_of_slot.shape[0]
    gram_matrix = lax.psum(partial_value, ("lat", "x", "core")) / (levels * slots * degrees)
    return (spectral.astype(jnp.bfloat16), gram_matrix)


class Rows:
    def __init__(self, fields, lat_dev):
        self.fields = fields
        self.rest = lat_dev % LANES
        self.pack = LANES // self.rest
        self.block = self.pack if fields % self.pack == 0 else fields
        self.blocks = fields // self.block
        self.quads_in = -(-self.block // self.pack)
        self.quads = self.blocks * self.quads_in
        self.width = (self.block + self.quads_in) * LANES
        self.total = self.blocks * self.width

    def full(self, f):
        return f // self.block * self.width + f % self.block * LANES

    def tail(self, q):
        return q // self.quads_in * self.width + (self.block + q % self.quads_in) * LANES

    def quad_of(self, f):
        inner = f % self.block
        return f // self.block * self.quads_in + inner // self.pack, inner % self.pack


def fourier_kernel(scale, rows, with_add, first, *refs):
    own = refs[: rows.block]
    if with_add:
        t0, t1, other, add, out = refs[rows.block :]
    else:
        t0, t1, other, out = refs[rows.block :]
    spare = rows.width - rows.block * other.shape[1]
    zero = [jnp.zeros((spare, other.shape[2]), other.dtype)] if spare else []
    whole = range(rows.block)
    g0 = [own[f][0, :LANES, :] for f in whole] + [own[f][0, LANES:, :] for f in whole]
    g1 = [other[f, :LANES, :] for f in whole] + [other[f, LANES:, :] for f in whole]
    dims = (((1,), (1,)), ((), ()))
    g0 = jnp.concatenate(g0 + zero, axis=0)
    g1 = jnp.concatenate(g1 + zero, axis=0)
    total = lax.dot_general(t0[...], g0, dims, preferred_element_type=jnp.float32)
    total += lax.dot_general(t1[...], g1, dims, preferred_element_type=jnp.float32)
    total *= scale
    if with_add:
        total += add[...].astype(jnp.float32)
    out[...] = total.astype(out.dtype)


def fourier(t0, t1, by_field, first, other, scale, rows, add=None):
    cols, lon = t0.shape
    lat_dev = other.shape[1]
    table = pl.BlockSpec((cols, lon), lambda i, at: (0, 0))
    own = [
        pl.BlockSpec((1, lat_dev, lon), lambda i, at, f=f: (at[0] + i * rows.block + f, 0, 0))
        for f in range(rows.block)
    ]
    field = pl.BlockSpec((rows.block, lat_dev, lon), lambda i, at: (i, 0, 0))
    wide = pl.BlockSpec((cols, rows.width), lambda i, at: (0, i))
    adds = [] if add is None else [add]
    return pl.pallas_call(
        functools.partial(fourier_kernel, scale, rows, add is not None),
        grid_spec=pltpu.PrefetchScalarGridSpec(
            num_scalar_prefetch=1,
            grid=(rows.blocks,),
            in_specs=own + [table, table, field] + [wide for _ in adds],
            out_specs=wide,
        ),
        out_shape=jax.ShapeDtypeStruct((cols, rows.total), jnp.bfloat16),
        compiler_params=pltpu.CompilerParams(vmem_limit_bytes=VMEM),
        cost_estimate=pl.CostEstimate(
            flops=4 * cols * rows.total * lon,
            bytes_accessed=4 * rows.total * lon + 4 * cols * rows.total + 4 * cols * lon,
            transcendentals=0,
        ),
        name="fourier",
    )(first.reshape(1), *[by_field] * rows.block, t0, t1, other, *adds)


def left_rows(bands, rows, cof):
    fields, pack, rest = rows.fields, rows.pack, rows.rest
    lane = lax.broadcasted_iota(jnp.int32, (CORES * rows.quads * SUB, LANES), 1) // rest

    def stacked(z, starts):
        parts = [
            cof[z * CORES + c, :, at : at + LANES].astype(jnp.float32)
            for c in range(CORES)
            for at in starts
        ]
        return jnp.concatenate(parts, axis=0)

    left = [stacked(z, [rows.full(f) for f in range(fields)]) for z in range(bands)]
    for g in range(bands // pack):
        shards = [None] * pack
        for slot in range(pack):
            tail = stacked(g * pack + slot, [rows.tail(q) for q in range(rows.quads)])
            for j in range(pack):
                shift = (slot - j) % pack * rest
                moved = tail if shift == 0 else pltpu.roll(tail, shift, 1)
                shards[j] = moved if slot == 0 else jnp.where(lane == slot, moved, shards[j])
        pieces = []
        for c in range(CORES):
            for f in range(fields):
                quad, j = rows.quad_of(f)
                at = (c * rows.quads + quad) * SUB
                pieces.append(shards[j][at : at + SUB])
        left.append(jnp.concatenate(pieces, axis=0))
    return jnp.concatenate(left, axis=1)


def legendre_kernel(bands, chunks, lat_dev, degrees, *refs):
    cofs = refs[: len(chunks)]
    leg, wave = refs[len(chunks) : len(chunks) + 2]
    outs = refs[len(chunks) + 2 :]
    left = [left_rows(bands, rows, cof) for rows, cof in zip(chunks, cofs, strict=True)]
    left = jnp.concatenate(left, axis=0)
    count = left.shape[0]
    slot_of_row = lax.broadcasted_iota(jnp.int32, (count, 1), 0) % SUB // 2
    total = jnp.zeros((count, degrees), jnp.float32)
    for s in range(SUB // 2):
        here = jnp.where(slot_of_row == s, left, 0.0).astype(jnp.bfloat16)
        table = jnp.concatenate(
            [leg[s, z * lat_dev : z * lat_dev + LANES, :] for z in range(bands)]
            + [leg[s, z * lat_dev + LANES : (z + 1) * lat_dev, :] for z in range(bands)],
            axis=0,
        )
        total += jnp.dot(here, table, preferred_element_type=jnp.float32)
    total = total.reshape(count // SUB, SUB, degrees)
    degree = lax.broadcasted_iota(jnp.int32, (SUB, degrees), 1)
    keep = degree >= wave[:, :1]
    total = jnp.where(keep[None], total, 0.0)
    at = 0
    for out in outs:
        out[...] = total[at : at + out.shape[0]].astype(out.dtype)
        at += out.shape[0]


def legendre_sums(cofs, chunks, leg, waves):
    sources, slot_rows, _ = cofs[0].shape
    slots, lats, degrees = leg.shape
    bands = sources // CORES
    lat_dev = lats // bands
    counts = [CORES * rows.fields for rows in chunks]
    total = sum(rows.total for rows in chunks)
    return pl.pallas_call(
        functools.partial(legendre_kernel, bands, chunks, lat_dev, degrees),
        grid=(slot_rows // SUB,),
        in_specs=[pl.BlockSpec((sources, SUB, rows.total), lambda i: (0, i, 0)) for rows in chunks]
        + [
            pl.BlockSpec((SUB // 2, lats, degrees), lambda i: (i, 0, 0)),
            pl.BlockSpec((SUB, LANES), lambda i: (i, 0)),
        ],
        out_specs=[pl.BlockSpec((n, SUB, degrees), lambda i: (0, i, 0)) for n in counts],
        out_shape=[jax.ShapeDtypeStruct((n, slot_rows, degrees), jnp.bfloat16) for n in counts],
        compiler_params=pltpu.CompilerParams(vmem_limit_bytes=VMEM),
        cost_estimate=pl.CostEstimate(
            flops=4 * sum(counts) * slot_rows * lats * degrees,
            bytes_accessed=2 * sources * slot_rows * total + 2 * slots * lats * degrees,
            transcendentals=0,
        ),
        name="legendre",
    )(*cofs, leg, waves)


def gram_kernel(groups, rows, vectors, *refs):
    specs = refs[:groups]
    weight, wave, place, before, out, total = refs[groups:]
    step = pl.program_id(0) * pl.num_programs(1) + pl.program_id(1)
    values = jnp.concatenate([r[...].reshape(-1, r.shape[-1]) for r in specs], axis=0)
    whole, degrees = values.shape
    old = whole - rows
    factor = jnp.where(wave[:, :1] == 0, 1.0, 2.0).astype(jnp.float32)
    scaled = values[old:].astype(jnp.float32).reshape(rows // SUB, SUB, degrees)
    scaled = scaled * (factor * weight[0])[None]
    scaled = scaled.reshape(rows, degrees).astype(jnp.bfloat16)
    part = lax.dot_general(
        scaled, values, (((1,), (1,)), ((), ())), preferred_element_type=jnp.float32
    )

    @pl.when(step == 0)
    def _():
        total[...] = part

    @pl.when(step > 0)
    def _():
        total[...] += part

    def mul(x, y):
        dims = (((1,), (1,)), ((), ()))
        return lax.dot_general(
            x, y, dims, preferred_element_type=jnp.float32, precision=lax.Precision.HIGHEST
        )

    @pl.when(step == pl.num_programs(0) * pl.num_programs(1) - 1)
    def _():
        row = lax.broadcasted_iota(jnp.int32, (rows, whole), 0)
        col = lax.broadcasted_iota(jnp.int32, (rows, whole), 1)
        kept = jnp.where(row % SUB == col % SUB, total[...], 0.0)
        slot = lax.broadcasted_iota(jnp.int32, (vectors, whole), 0)
        pick = (place[:1, :] == slot).astype(jnp.float32)
        seen = lax.broadcasted_iota(jnp.int32, (vectors, whole), 1)
        ours = jnp.where(seen < old, 0.0, pick)[:, old:] if old else pick
        across = mul(pick, kept)
        found = before[...] + mul(ours, across)
        if old:
            found += mul(mul(jnp.where(seen < old, pick, 0.0), kept), ours)
        out[...] = found


def gram_sums(specs, order, last, vectors, before, weight, waves):
    _, levels, slot_rows, degrees = specs[0].shape
    rows = len(order) * SUB
    place = jnp.repeat(jnp.asarray(order, jnp.int32), SUB)
    place = jnp.broadcast_to(place[None], (SUB, rows))
    square = pl.BlockSpec((vectors, vectors), lambda l, i: (0, 0))
    return pl.pallas_call(
        functools.partial(gram_kernel, len(specs), last * SUB, vectors),
        grid=(levels, slot_rows // SUB),
        in_specs=[
            pl.BlockSpec((s.shape[0], 1, SUB, degrees), lambda l, i: (0, l, i, 0)) for s in specs
        ]
        + [
            pl.BlockSpec((1, 1, degrees), lambda l, i: (l, 0, 0)),
            pl.BlockSpec((SUB, LANES), lambda l, i: (i, 0)),
            pl.BlockSpec((SUB, rows), lambda l, i: (0, 0)),
            square,
        ],
        out_specs=square,
        out_shape=jax.ShapeDtypeStruct((vectors, vectors), jnp.float32),
        scratch_shapes=[pltpu.VMEM((last * SUB, rows), jnp.float32)],
        compiler_params=pltpu.CompilerParams(vmem_limit_bytes=VMEM),
        name="gram",
    )(*specs, weight.reshape(levels, 1, degrees), waves, place, before)


def chunk_sizes(half, quad):
    ramp = half % quad + quad
    return [ramp // 2, ramp - ramp // 2] + [quad] * ((half - ramp) // quad)


def groups_of(count):
    pairs = [list(range(i, min(i + 2, count - 1))) for i in range(0, count - 1, 2)]
    return pairs + [[count - 1]]


def cosine(turn, total):
    inside = turn - jnp.floor(turn * (1.0 / total) + 0.5) * total
    angle = inside * (2.0 * math.pi / total)
    square = angle * angle
    value = 1.0 / math.factorial(18)
    for k in range(8, -1, -1):
        value = 1.0 / math.factorial(2 * k) - square * value
    return value


def make_tables(waves, here, lon_total):
    part = jnp.arange(waves.shape[0] * 2, dtype=jnp.int32) % 2
    quarter = part.astype(jnp.float32) * (lon_total / 4.0)
    turn = jnp.repeat(waves, 2).astype(jnp.float32)[:, None] * here[None, :] + quarter[:, None]
    return cosine(turn, float(lon_total)).astype(jnp.bfloat16)


def all_sum(value):
    for axis in ("core", "x", "lat"):
        size = lax.axis_size(axis)
        step = 1
        while step < size:
            value = value + lax.ppermute(value, axis, [(i, i ^ step) for i in range(size)])
            step *= 2
    return value


def after(value, other):
    return lax.optimization_barrier((value, other))[0]


def fast(grid_fields, legendre, wave_of_slot, energy_weight):
    lat_dev, vectors, levels, lon_dev = grid_fields.shape
    bands = lax.axis_size("lat")
    xs = lax.axis_size("x")
    lon_total = lon_dev * xs * CORES
    per_dev, _, degrees = legendre.shape
    slots = wave_of_slot.shape[0]
    scale = 1.0 / math.sqrt(lon_total)
    half = vectors // CORES
    my_core = lax.axis_index("core")
    my_x = lax.axis_index("x")
    by_field = grid_fields.transpose(1, 2, 0, 3).reshape(vectors * levels, lat_dev, lon_dev)
    swap = [(0, 1), (1, 0)]
    pack = LANES // (lat_dev % LANES)
    sizes = chunk_sizes(half, pack // math.gcd(pack, levels))
    starts = [sum(sizes[:i]) for i in range(len(sizes))]
    chunks = [Rows(size * levels, lat_dev) for size in sizes]
    groups = groups_of(len(sizes))

    waves = wave_of_slot.reshape(bands, xs, CORES * per_dev).transpose(1, 0, 2).reshape(xs, -1)
    waves = jnp.roll(waves, -my_x, axis=0)
    longitude = jnp.arange(lon_dev, dtype=jnp.int32)
    sectors = [
        ((my_x * CORES + core) * lon_dev + longitude).astype(jnp.float32)
        for core in (my_core, 1 - my_core)
    ]
    tables = {s: [make_tables(waves[s], here, lon_total) for here in sectors] for s in range(1, xs)}
    device_slot = lax.axis_index(("lat", "x", "core")) * per_dev
    own_waves = lax.dynamic_slice_in_dim(wave_of_slot, device_slot, per_dev, 0)
    wave_rows = jnp.broadcast_to(jnp.repeat(own_waves, 2)[:, None], (2 * per_dev, LANES))

    sent = []
    cofs = []
    done = {}
    for i, rows in enumerate(chunks):
        first = (my_core * half + starts[i]) * levels
        away = ((1 - my_core) * half + starts[i]) * levels
        if sent:
            away = after(away, sent[max(i - 2, 0)])
        away = lax.dynamic_slice_in_dim(by_field, away, rows.fields, 0)
        came = lax.ppermute(away, "core", swap)
        add = None
        for step in range(1, xs):
            there = fourier(*tables[step], by_field, first, came, scale, rows)
            part = lax.ppermute(there, "x", [(j, (j + step) % xs) for j in range(xs)])
            add = part if xs == 2 else part.astype(jnp.float32) + (0.0 if add is None else add)
        if not sent:
            own_set = after(waves[0], there)
            tables[0] = [make_tables(own_set, here, lon_total) for here in sectors]
        sent.append(there)
        mine = fourier(*tables[0], by_field, first, came, scale, rows, add)
        mine = mine.reshape(bands * CORES, 2 * per_dev, -1)
        if cofs:
            mine = after(mine, cofs[-1])
        cofs.append(lax.all_to_all(mine, ("lat", "core"), 0, 0, tiled=True))
        for group in groups:
            if group[-1] == i:
                sums = legendre_sums(
                    [cofs[j] for j in group], [chunks[j] for j in group], legendre, wave_rows
                )
                for j, value in zip(group, sums, strict=True):
                    done[j] = value.reshape(-1, levels, 2 * per_dev, degrees)
    done = [done[i] for i in range(len(chunks))]
    order = [
        c * half + start + k
        for size, start in zip(sizes, starts, strict=True)
        for c in range(CORES)
        for k in range(size)
    ]
    shape = (CORES, -1, levels, per_dev, 2, degrees)
    spectral = jnp.concatenate([d.reshape(shape) for d in done], axis=1)
    tail = CORES * sizes[-1]
    grams = functools.partial(gram_sums, vectors=vectors, weight=energy_weight, waves=wave_rows)
    empty = jnp.zeros((vectors, vectors), jnp.float32)
    partial_value = grams(done[:-1], order[:-tail], vectors - tail, before=empty)
    partial_value = grams(done, order, tail, before=partial_value)
    gram_matrix = all_sum(partial_value) / (levels * slots * degrees)
    return (spectral.reshape(vectors, levels, per_dev, 2, degrees), gram_matrix)


def on_device(grid_fields, legendre, wave_of_slot, energy_weight):
    lat_dev, vectors, _, lon_dev = grid_fields.shape
    bands = lax.axis_size("lat")
    rest = lat_dev % LANES
    fits = (
        lat_dev // LANES == 1
        and rest >= 16
        and LANES % rest == 0
        and bands % (LANES // rest) == 0
        and legendre.shape[0] * 2 % SUB == 0
        and vectors % CORES == 0
        and lon_dev % LANES == 0
        and wave_of_slot.shape[0] * lon_dev * lax.axis_size("x") * CORES < 2**23
        and lax.axis_size("x") > 1
        and all(lax.axis_size(a) & (lax.axis_size(a) - 1) == 0 for a in ("lat", "x", "core"))
    )
    body = fast if fits else plain
    return body(grid_fields, legendre, wave_of_slot, energy_weight)


def solution(mesh):
    lat, lon = mesh.devices.shape
    wide = Mesh(mesh.devices.reshape(lat, lon // CORES, CORES), ("lat", "x", "core"))
    lons = ("x", "core")
    placed = (P("lat", None, None, lons), P(("lat", "x", "core"), None, None), P(), P())
    return jax.shard_map(
        on_device,
        mesh=wide,
        in_specs=placed,
        out_specs=(P(None, None, ("lat", "x", "core"), None, None), P()),
        check_vma=False,
    )
```
